32 devices in a mesh: twin: 2 (over y), gx: 4 (over z), gy: 2 (over core), gz: 2 (over x).
Axes of the slice: x: 2, y: 2, z: 4, core: 2. Of those that a mesh axis runs over, the one named last changes fastest.
Arguments:
- potential: float32 [64, 32, 256], P(('twin', 'gx'), 'gy', 'gz'), parts along dimension 0, may hold values from 0 to 1
- gating: float32 [64, 32, 256], P(('twin', 'gx'), 'gy', 'gz'), parts along dimension 0, may hold values from 0 to 1
- adjoint_v: float32 [64, 32, 256], P(('twin', 'gx'), 'gy', 'gz'), parts along dimension 0, may hold values from -6 to 6
- adjoint_h: float32 [64, 32, 256], P(('twin', 'gx'), 'gy', 'gz'), parts along dimension 0, may hold values from -6 to 6
- recorded: float32 [64, 32, 256], P(('twin', 'gx'), 'gy', 'gz'), parts along dimension 0, may hold values from 0 to 1
- tissue_mask: int32 [64, 32, 256], P(('twin', 'gx'), 'gy', 'gz'), parts along dimension 0, may hold values from 0 to 1
- fibre_sector: int32 [64, 32, 256], P(('twin', 'gx'), 'gy', 'gz'), parts along dimension 0, may hold values from 0 to 11
- region_label: int32 [64, 32, 256], P(('twin', 'gx'), 'gy', 'gz'), parts along dimension 0, may hold values from 0 to 15
- fibre_table: float32 [24, 9], P('twin'), parts along dimension 0, may hold values from 0.005 to 0.025
- conductance: float32 [32], P('twin'), parts along dimension 0, may hold values from 0.5 to 2
Outputs:
- lambda_v: float32 [64, 32, 256], P(('twin', 'gx'), 'gy', 'gz'), parts along dimension 0
- lambda_h: float32 [64, 32, 256], P(('twin', 'gx'), 'gy', 'gz'), parts along dimension 0
- sensitivity: float32 [32], P('twin'), parts along dimension 0
The draws below stay inside these ranges and needn't reach their ends.
There are 2 independent parts, one for each index of `twin`. The reference program is written for one: setup_inputs(seed, part) draws one part's arguments, and reference() takes and returns one part's arrays. A program takes and returns all parts, laid end to end along the dimension named above; each array names one. Nothing has to cross between parts.
All inputs are finite; a program needn't handle non-finite values.
Results may differ from the reference program's by a relative error of at most 0.0003.
Values sent between devices are 32-bit elements; how exact they have to be, the bound alone decides.
No kernel may reach another device: no remote copies, remote signals or barrier semaphores. Data moves between devices by JAX's collectives and lax.ppermute only.
A program may use at most 64 MiB of HBM per device.

```python
import math
import jax
import jax.numpy as jnp

WINDOW_STEPS = 3
SECTORS = 12
REGIONS = 16
NX = 32
NY = 32
NZ = 256


def draw_tissue_mask(key, part):
    local = jax.random.fold_in(key, 17)
    xs = jnp.arange(NX, dtype=jnp.int32)[:, None, None]
    ys = jnp.arange(NY, dtype=jnp.int32)[None, :, None]
    zs = jnp.arange(NZ, dtype=jnp.int32)[None, None, :]
    coord_x = (2 * xs + 1 - NX) * 1000 // NX
    coord_y = (2 * ys + 1 - NY) * 1000 // NY
    coord_z = (2 * zs + 1 - NZ) * 1000 // NZ
    radial = coord_y * coord_y + coord_z * coord_z
    outer = coord_x * coord_x + radial < 950 * 950
    cavity_left = (coord_x + 300) * (coord_x + 300) + radial < 450 * 450
    cavity_right = (coord_x - 350) * (coord_x - 350) + radial < 330 * 330
    holes = jax.random.randint(local, (NX, NY, NZ), 0, 10) > 0
    inside = outer & jnp.logical_not(cavity_left) & jnp.logical_not(cavity_right) & holes
    return jnp.where(inside, 1, 0).astype(jnp.int32)


def draw_region_label(key, part):
    local = jax.random.fold_in(key, 29)
    xs = jnp.arange(NX, dtype=jnp.int32)[:, None, None]
    slab = xs * (REGIONS // 2) // NX
    extra = jax.random.randint(local, (NX, NY, NZ), 0, 2)
    return (slab * 2 + extra).astype(jnp.int32)


def place_ends(drawn, own_key, smallest, top_value):
    longest = drawn.shape.index(max(drawn.shape))
    spots = []
    for shift in (0, 1):
        where = [jax.random.randint(jax.random.fold_in(own_key, axis), (), 0, length) for axis, length in enumerate(drawn.shape)]
        where[longest] = (where[longest] + shift) % drawn.shape[longest]
        spots.append(tuple(where))
    return drawn.at[spots[0]].set(smallest).at[spots[1]].set(top_value)


def block_scale(own_key, dims, pieces, low, largest):
    def one(axis_at, blocks):
        heights = jax.random.uniform(jax.random.fold_in(jax.random.fold_in(own_key, 6), axis_at), (blocks,), jnp.float32, low / len(pieces), largest / len(pieces))
        return jnp.repeat(jnp.exp(heights), dims[axis_at] // blocks).reshape((-1,) + (1,) * (len(dims) - axis_at - 1))

    gain = one(*pieces[0])
    for cut in pieces[1:]:
        gain = gain * one(*cut)
    return gain


def noise(stream_key, shape, deviation, most, shards=(), kind=jnp.bfloat16):
    result = deviation * jax.random.normal(stream_key, shape, jnp.float32)
    if shards:
        result = result * block_scale(stream_key, shape, shards, -0.22, 0.18)
    return jnp.clip(result, -most, most).astype(kind)


def setup_inputs(seed: int = 0, part: int = 0) -> dict:
    keys = jax.random.split(jax.random.key(seed), 11)
    own_keys = jax.random.split(jax.random.fold_in(keys[10], part), 11)
    return {
        "potential": jnp.clip(1.0 * jax.random.uniform(own_keys[0], (NX, NY, NZ), jnp.float32) ** block_scale(own_keys[0], (NX, NY, NZ), ((0, 4), (1, 2), (2, 2)), -0.2, 0.2), 0.0, 1.0),
        "gating": jnp.clip(1.0 * jax.random.uniform(own_keys[1], (NX, NY, NZ), jnp.float32) ** block_scale(own_keys[1], (NX, NY, NZ), ((0, 4), (1, 2), (2, 2)), -0.2, 0.2), 0.0, 1.0),
        "adjoint_v": noise(own_keys[2], (NX, NY, NZ), 1.0, 6.0, ((0, 4), (1, 2), (2, 2)), jnp.float32),
        "adjoint_h": noise(own_keys[3], (NX, NY, NZ), 1.0, 6.0, ((0, 4), (1, 2), (2, 2)), jnp.float32),
        "recorded": jnp.clip(1.0 * jax.random.uniform(own_keys[4], (NX, NY, NZ), jnp.float32) ** block_scale(own_keys[4], (NX, NY, NZ), ((0, 4), (1, 2), (2, 2)), -0.2, 0.2), 0.0, 1.0),
        "tissue_mask": draw_tissue_mask(jax.random.fold_in(jax.random.fold_in(keys[10], part), 71), part),
        "fibre_sector": place_ends(jax.random.randint(own_keys[6], (NX, NY, NZ), 0, SECTORS), jax.random.fold_in(own_keys[6], 1), 0, SECTORS - 1).astype(jnp.int32),
        "region_label": draw_region_label(jax.random.fold_in(jax.random.fold_in(keys[10], part), 71), part),
        "fibre_table": jnp.clip(jnp.exp(jax.random.uniform(own_keys[8], (SECTORS, 9), jnp.float32, math.log(0.005), math.log(0.025))), 0.005, 0.025),
        "conductance": jnp.clip(jnp.exp(jax.random.uniform(own_keys[9], (REGIONS,), jnp.float32, math.log(0.5), math.log(2.0))), 0.5, 2.0),
    }


step_size = 0.1
tau_inward = 0.3
tau_outward = 6.0
tau_opening = 12.0
tau_closing = 15.0
gate_level = 0.13
gate_width = 0.02
gradient_gain = 30.0
PAIR_OFFSETS = ((1, 0, 0), (0, 1, 0), (0, 0, 1), (1, 1, 0), (1, -1, 0), (1, 0, 1), (1, 0, -1), (0, 1, 1), (0, 1, -1))

def crop(array, trim):
    if trim == 0:
        return array
    return array[..., trim:-trim, trim:-trim, trim:-trim]

def shifted(padded, offset):
    sizes = [padded.shape[-3 + axis] - 2 for axis in range(3)]
    starts = [1 + offset[axis] for axis in range(3)]
    return padded[..., starts[0]:starts[0] + sizes[0], starts[1]:starts[1] + sizes[1], starts[2]:starts[2] + sizes[2]]

def neighbour_terms(field_pad, tissue_pad, flux_pad):
    centre = crop(field_pad, 1)
    tissue_mid = crop(tissue_pad, 1)
    flux_mid = crop(flux_pad, 1)
    total = jnp.zeros_like(centre)
    for direction, base in enumerate(PAIR_OFFSETS):
        for sign in (1, -1):
            offset = tuple((sign * part for part in base))
            coupling = 0.5 * (flux_mid[direction] * shifted(tissue_pad, offset) + shifted(flux_pad[direction], offset) * tissue_mid)
            total = total + coupling * (shifted(field_pad, offset) - centre)
    return total

def region_terms(adjoint_pad, field_pad, tissue_pad, fibre_mid):
    adjoint_mid = crop(adjoint_pad, 1)
    centre = crop(field_pad, 1)
    total = jnp.zeros_like(centre)
    for direction, base in enumerate(PAIR_OFFSETS):
        for sign in (1, -1):
            offset = tuple((sign * part for part in base))
            weight = shifted(tissue_pad, offset) * fibre_mid[direction]
            total = total + weight * (shifted(adjoint_pad, offset) - adjoint_mid) * (shifted(field_pad, offset) - centre)
    return -0.5 * crop(tissue_pad, 1) * total

def ionic(volts, gate_now):
    switch = jax.nn.sigmoid((volts - gate_level) / gate_width)
    drive_v = gate_now * volts * volts * (1.0 - volts) / tau_inward - volts / tau_outward
    drive_h = (1.0 - switch) * (1.0 - gate_now) / tau_opening - switch * gate_now / tau_closing
    return (drive_v, drive_h)

def ionic_partials(volts, gate_now):
    switch = jax.nn.sigmoid((volts - gate_level) / gate_width)
    slope = switch * (1.0 - switch) / gate_width
    deriv_vv = gate_now * (2.0 * volts - 3.0 * volts * volts) / tau_inward - 1.0 / tau_outward
    deriv_vh = volts * volts * (1.0 - volts) / tau_inward
    deriv_hv = slope * (-(1.0 - gate_now) / tau_opening - gate_now / tau_closing)
    deriv_hh = -(1.0 - switch) / tau_opening - switch / tau_closing
    return (deriv_vv, deriv_vh, deriv_hv, deriv_hh)

def forward_step(volts_pad, gate_now, tissue_mid, tissue_pad, flux_pad):
    volts = crop(volts_pad, 1)
    drive_v, drive_h = ionic(volts, gate_now)
    spread = neighbour_terms(volts_pad, tissue_pad, flux_pad)
    return (volts + tissue_mid * (spread + step_size * drive_v), gate_now + tissue_mid * step_size * drive_h)

def reference(potential, gating, adjoint_v, adjoint_h, recorded, tissue_mask, fibre_sector, region_label, fibre_table, conductance):
    fields = jnp.stack([tissue_mask, fibre_sector, region_label])
    fields_pad = jnp.pad(fields, ((0, 0), (1, 1), (1, 1), (1, 1)))
    tissue_pad = fields_pad[0].astype(jnp.float32)
    fibre_pad = jnp.moveaxis(fibre_table[fields_pad[1]], -1, 0)
    flux_pad = (tissue_pad * conductance[fields_pad[2]])[None] * fibre_pad
    tissue_mid = crop(tissue_pad, 1)
    fibre_mid = crop(fibre_pad, 1)
    volts, gate_now = (potential, gating)
    saved_pads = []
    saved_gates = []
    for step in range(WINDOW_STEPS):
        volts_pad = jnp.pad(volts, 1)
        saved_pads.append(volts_pad)
        saved_gates.append(gate_now)
        volts, gate_now = forward_step(volts_pad, gate_now, tissue_mid, tissue_pad, flux_pad)
    back_v = adjoint_v + tissue_mid * (volts - recorded)
    back_h = adjoint_h
    total = jnp.zeros((REGIONS,), jnp.float32)
    for step in reversed(range(WINDOW_STEPS)):
        masked = tissue_mid * back_v
        masked_pad = jnp.pad(masked, 1)
        volts_pad = saved_pads[step]
        terms = region_terms(masked_pad, volts_pad, tissue_pad, fibre_mid)
        total = total + jax.ops.segment_sum(terms.ravel(), region_label.ravel(), num_segments=REGIONS)
        deriv_vv, deriv_vh, deriv_hv, deriv_hh = ionic_partials(crop(volts_pad, 1), saved_gates[step])
        spread = neighbour_terms(masked_pad, tissue_pad, flux_pad)
        next_v = back_v + spread + step_size * tissue_mid * (deriv_vv * back_v + deriv_hv * back_h)
        next_h = back_h + step_size * tissue_mid * (deriv_vh * back_v + deriv_hh * back_h)
        back_v, back_h = (next_v, next_h)
    scale = gradient_gain / math.sqrt(NX * NY * NZ / REGIONS)
    return (back_v, back_h, total * scale)
```

```python
import functools
import math

import jax
import jax.numpy as jnp
from jax import lax
from jax.experimental import pallas as pl
from jax.experimental.pallas import tpu as pltpu
from jax.sharding import PartitionSpec as P

WINDOW_STEPS = 3
HALO = 2 * WINDOW_STEPS
LANES = 128
TILE = 8

step_size = 0.1
tau_inward = 0.3
tau_outward = 6.0
tau_opening = 12.0
tau_closing = 15.0
gate_level = 0.13
gate_width = 0.02
gradient_gain = 30.0
PAIR_OFFSETS = (
    (1, 0, 0),
    (0, 1, 0),
    (0, 0, 1),
    (1, 1, 0),
    (1, -1, 0),
    (1, 0, 1),
    (1, 0, -1),
    (0, 1, 1),
    (0, 1, -1),
)
DIRS = len(PAIR_OFFSETS)
Z_DIRS = tuple(d for d, o in enumerate(PAIR_OFFSETS) if o[2])
Y_DIRS = tuple(d for d, o in enumerate(PAIR_OFFSETS) if o[1])
V, G, S, H, B, A = range(6)
WIDTHS = (HALO, HALO, HALO, HALO - 1, WINDOW_STEPS, WINDOW_STEPS - 1)
STARTS = tuple(sum(WIDTHS[:f]) for f in range(6))
PLANES = sum(WIDTHS)
SLOT = 16


def matchings(count):
    result = []
    for parity in range(0 if count == 1 else 1 if count == 2 else 2):
        partner = [i + 1 if i % 2 == parity else i - 1 for i in range(count)]
        result.append([j if 0 <= j < count else i for i, j in enumerate(partner)])
    return result


def looks_up(axis, parity):
    return lax.rem(lax.axis_index(axis), 2) == parity


def lane_ids(rows):
    return lax.broadcasted_iota(jnp.int32, (rows, LANES), 1)


def aligned(start):
    return start if isinstance(start, int) else pl.multiple_of(start, TILE)


def pack_kernel(nx, cond, pot, gat, adv, adh, rec, mask, sec, reg, *outs):
    sx, (sz,) = outs[:nx], outs[nx : nx + 1]
    sd = outs[nx + 1 : 2 * nx + 1]
    sy, g_out, s_out, b_out = outs[2 * nx + 1 :]
    X, Y, _ = pot.shape
    core = lax.axis_index("gy")
    label = reg[...]
    factor = jnp.zeros(label.shape, jnp.float32)
    for r in range(cond.shape[0]):
        factor = jnp.where(label == r, cond[r], factor)
    m = mask[...].astype(jnp.float32)
    g_out[...] = m * factor
    s_out[...] = sec[...].astype(jnp.float32)
    b_out[...] = adv[...] - m * rec[...]
    fields = (pot, g_out, s_out, gat, b_out, adh)
    for k in range(nx):
        up = looks_up("gx", k)
        for f, w in enumerate(WIDTHS):
            start = jnp.where(up, X - w, 0)
            sx[k][STARTS[f] : STARTS[f] + w] = fields[f][pl.ds(start, w)]
    send_row = pl.multiple_of(TILE * (1 - core), TILE)
    half = Y // 2
    lanes = lane_ids(X * Y)
    packed = pot[...].reshape(X * Y, LANES)
    for f in range(1, 6):
        rolled = pltpu.roll(fields[f][...].reshape(X * Y, LANES), SLOT * f, 1)
        inside = (lanes >= SLOT * f - SLOT // 2) & (lanes < SLOT * f + SLOT // 2)
        packed = jnp.where(inside, rolled, packed)
    sz[...] = packed.reshape(X, Y, LANES)
    for k in range(nx):
        start = jnp.where(looks_up("gx", k), X - HALO, 0)
        sd[k][...] = sz[pl.ds(start, HALO)]
    row = pl.multiple_of(jnp.where(core == 0, Y - TILE, 0), TILE)
    for f in range(6):
        sy[f] = fields[f][:, pl.ds(row, TILE), :]


def z_up(a, h):
    last = lane_ids(a.shape[0]) == LANES - 1
    ra, rh = pltpu.roll(a, LANES - 1, 1), pltpu.roll(h, LANES - 1, 1)
    return jnp.where(last, rh, ra), jnp.where(last, ra, rh)


def z_down(a, h):
    first = lane_ids(a.shape[0]) == 0
    ra, rh = pltpu.roll(a, 1, 1), pltpu.roll(h, 1, 1)
    return jnp.where(first, rh, ra), jnp.where(first, ra, rh)


def window_kernel(nx, nz, sizes, *refs):
    size_x, size_z = sizes
    it = iter(refs)

    def take(n):
        return [next(it) for _ in range(n)]

    tab, reg = take(2)
    own = take(6)
    rx, rz, rd = take(nx), take(nz), take(nx * nz)
    (yo,) = take(1)
    yx, yz, yd = take(nx), take(nz), take(nx * nz)
    out_v, out_h, out_t = take(3)
    U, MU, MK, FL, FZ, K, KZ = take(7)
    EG, ES, EH, EB, EA, SG, AV, AH, Q, RS = take(10)

    X, Y, _ = own[V].shape
    XE, YE = X + 2 * HALO, Y + TILE
    ROW = YE + TILE
    core = lax.axis_index("gy")
    xi, zi = lax.axis_index("gx"), lax.axis_index("gz")
    ro = pl.multiple_of(TILE * core, TILE)
    po = pl.multiple_of(Y * (1 - core), TILE)
    ps = pl.multiple_of((Y - TILE) * 0 + TILE * core * ((Y - TILE) // TILE), TILE)

    def at(x, row=0):
        return aligned(x * ROW + TILE + row)

    def load(ref, index, x, dy=0, rows=None, row=0):
        start = x * ROW + TILE + row + dy
        if not dy:
            start = aligned(start)
        return ref[index + (pl.ds(start, rows or YE), slice(None))]

    blank = jnp.zeros((TILE, LANES), jnp.float32)

    @pl.loop(0, XE + 1)
    def _(x):
        row = pl.multiple_of(x * ROW, TILE)
        for part in range(2):
            for kind in range(3):
                for n in range(WINDOW_STEPS):
                    U[n, kind, part, pl.ds(row, TILE), :] = blank
                    MU[n, kind, part, pl.ds(row, TILE), :] = blank
                MK[kind, part, pl.ds(row, TILE), :] = blank
            for d in Y_DIRS:
                K[d, part, pl.ds(row, TILE), :] = blank
            for i, d in enumerate(Z_DIRS):
                if d in Y_DIRS:
                    KZ[i, part, pl.ds(row, TILE), :] = blank

    stores = {G: EG, S: ES, H: EH, B: EB, A: EA}

    def put(f, part, xe, row, value):
        rows = value.shape[0]
        if f == V:
            U[0, 0, part, pl.ds(at(xe, row), rows), :] = value
        elif f == H:
            EH[0, part, xe, pl.ds(row, rows), :] = value
        else:
            stores[f][part, xe, pl.ds(row, rows), :] = value

    def spread(f, packs):
        parts = [pltpu.roll(p, (LANES - SLOT * f) % LANES, 1) if f else p for p in packs]
        if len(parts) == 1:
            value = parts[0]
        else:
            value = jnp.where(lane_ids(parts[0].shape[0]) < LANES // 2, *[
                jnp.where(looks_up("gz", 0), parts[0], parts[1]),
                jnp.where(looks_up("gz", 0), parts[1], parts[0]),
            ])
        return value

    def lanes_ok(rows):
        lanes = lane_ids(rows)
        right = (lanes < HALO) & (zi < size_z - 1)
        left = (lanes >= LANES - HALO) & (zi > 0)
        return right | left

    if nx < 2 or nz < 1:
        for ref in (EG, ES, EB, EA):
            ref[...] = jnp.zeros(ref.shape, jnp.float32)
        EH[0] = jnp.zeros(EH.shape[1:], jnp.float32)
        for part in range(2):
            U[0, 0, part] = jnp.zeros(U.shape[3:], jnp.float32)

    for f, w in enumerate(WIDTHS):
        for i in range(X):
            put(f, 0, HALO + i, ro, own[f][i])
            put(f, 0, HALO + i, po, yo[f, i])
        for k in range(nx):
            up = looks_up("gx", k)
            ok = jnp.where(up, xi < size_x - 1, xi > 0)
            dest = jnp.where(up, HALO + X, HALO - w)
            for i in range(w):
                mine = rx[k][STARTS[f] + i]
                theirs = yx[k][STARTS[f] + i, pl.ds(ps, TILE), :]
                if f == G:
                    mine, theirs = jnp.where(ok, mine, 0.0), jnp.where(ok, theirs, 0.0)
                put(f, 0, dest + i, ro, mine)
                put(f, 0, dest + i, po, theirs)

    if nz:

        def halo_plane(xe, ok, mine, theirs):
            for f in range(6):
                a, b = spread(f, mine), spread(f, theirs)
                if f == G:
                    a = jnp.where(lanes_ok(Y) & ok, a, 0.0)
                    b = jnp.where(lanes_ok(TILE) & ok, b, 0.0)
                put(f, 1, xe, ro, a)
                put(f, 1, xe, po, b)

        @pl.loop(0, X)
        def _(i):
            halo_plane(
                HALO + i, True, [r[i] for r in rz], [r[i, pl.ds(ps, TILE), :] for r in yz]
            )

        @pl.loop(0, HALO)
        def _(i):
            for k in range(nx):
                up = looks_up("gx", k)
                ok = jnp.where(up, xi < size_x - 1, xi > 0)
                dest = jnp.where(up, HALO + X, 0)
                halo_plane(
                    dest + i,
                    ok,
                    [r[i] for r in rd[k * nz : (k + 1) * nz]],
                    [r[i, pl.ds(ps, TILE), :] for r in yd[k * nz : (k + 1) * nz]],
                )

    def put_kinds(ref, index, x, a, h):
        rows = pl.ds(at(x), YE)
        for kind, (p, q) in enumerate(((a, h), z_up(a, h), z_down(a, h))):
            ref[index + (kind, 0, rows, slice(None))] = p
            ref[index + (kind, 1, rows, slice(None))] = q

    @pl.loop(0, XE)
    def _(x):
        rows = pl.ds(at(x), YE)
        v = [load(U, (0, 0, part), x) for part in range(2)]
        for kind, pair in ((1, z_up(*v)), (2, z_down(*v))):
            for part in range(2):
                U[0, kind, part, rows, :] = pair[part]
        g = [EG[part, x] for part in range(2)]
        put_kinds(MK, (), x, *[jnp.where(t > 0.0, 1.0, 0.0) for t in g])
        sector = [
            jnp.where(g[part] > 0.0, ES[part, x], 0.0).astype(jnp.int32) for part in range(2)
        ]
        for d, (_, _, dz) in enumerate(PAIR_OFFSETS):
            line = jnp.broadcast_to(tab[d : d + 1, :], (YE, LANES))
            flux = [
                g[part] * jnp.take_along_axis(line, sector[part], axis=1) for part in range(2)
            ]
            for part in range(2):
                FL[d, part, rows, :] = flux[part]
            if dz:
                pair = (z_up if dz > 0 else z_down)(*flux)
                for part in range(2):
                    FZ[Z_DIRS.index(d), part, rows, :] = pair[part]

    def kind_of(dz):
        return 0 if dz == 0 else 1 if dz > 0 else 2

    @pl.loop(0, XE - 1)
    def _(x):
        rows = pl.ds(at(x), YE)
        for d, (dx, dy, dz) in enumerate(PAIR_OFFSETS):
            pair = []
            for part in range(2):
                both = load(MK, (0, part), x) * load(MK, (kind_of(dz), part), x + dx, dy)
                there = (
                    load(FZ, (Z_DIRS.index(d), part), x + dx, dy)
                    if dz
                    else load(FL, (d, part), x + dx, dy)
                )
                pair.append(jnp.where(both > 0.0, load(FL, (d, part), x) + there, 0.0))
                K[d, part, rows, :] = pair[part]
            if dz:
                back = (z_down if dz > 0 else z_up)(*pair)
                for part in range(2):
                    KZ[Z_DIRS.index(d), part, rows, :] = back[part]

    def spread_of(ref, index, x, part, rows=None, row=0):
        centre = load(ref, index + (0, part), x, 0, rows, row)
        total = None
        for d, (dx, dy, dz) in enumerate(PAIR_OFFSETS):
            up = load(ref, index + (kind_of(dz), part), x + dx, dy, rows, row)
            term = load(K, (d, part), x, 0, rows, row) * (up - centre)
            total = term if total is None else total + term
            down = load(ref, index + (kind_of(-dz), part), x - dx, -dy, rows, row)
            back = (
                load(KZ, (Z_DIRS.index(d), part), x - dx, -dy, rows, row)
                if dz
                else load(K, (d, part), x - dx, -dy, rows, row)
            )
            total = total + back * (down - centre)
        return centre, total

    for n in range(WINDOW_STEPS):
        reach = HALO - 1 - n
        last = n == WINDOW_STEPS - 1

        @pl.loop(HALO - reach, HALO + X + reach)
        def _(x, n=n, last=last):
            fresh = []
            for part in range(2):
                m = load(MK, (0, part), x)
                v, flow = spread_of(U, (n,), x, part)
                h = EH[n, part, x]
                s = jax.nn.sigmoid((v - gate_level) * (1.0 / gate_width))
                SG[n, part, x] = s
                drive = h * v * v * (1.0 - v) * (1.0 / tau_inward) - v * (1.0 / tau_outward)
                v_new = v + m * (flow + step_size * drive)
                if last:
                    a = EB[part, x] + m * v_new
                    AV[part, x] = a
                    fresh.append(m * a)
                else:
                    drive = (1.0 - s) * (1.0 - h) * (1.0 / tau_opening) - s * h * (
                        1.0 / tau_closing
                    )
                    EH[n + 1, part, x] = h + m * (step_size * drive)
                    fresh.append(v_new)
            if last:
                put_kinds(MU, (n,), x, *fresh)
            else:
                put_kinds(U, (n + 1,), x, *fresh)

    def terms():
        row = ro

        @pl.loop(0, X)
        def _(i):
            x = HALO + i
            mu = [load(MU, (n, 0, 0), x, 0, Y, row) for n in range(WINDOW_STEPS)]
            v = [load(U, (n, 0, 0), x, 0, Y, row) for n in range(WINDOW_STEPS)]
            total = jnp.zeros((Y, LANES), jnp.float32)
            for d, (dx, dy, dz) in enumerate(PAIR_OFFSETS):
                edge = None
                for sign in (1, -1):
                    index = (kind_of(sign * dz), 0)
                    where = (x + sign * dx, sign * dy, Y, row)
                    part = None
                    for n in range(WINDOW_STEPS):
                        term = (load(MU, (n,) + index, *where) - mu[n]) * (
                            load(U, (n,) + index, *where) - v[n]
                        )
                        part = term if part is None else part + term
                    part = part * load(MK, index, *where)
                    edge = part if edge is None else edge + part
                total = total + load(FL, (d, 0), x, 0, Y, row) * edge
            Q[i] = total

        RS[...] = jnp.zeros(RS.shape, jnp.float32)
        label = reg[...]
        for r in range(out_t.shape[0] * 0 + RS.shape[0] // TILE):
            found = jnp.where(label == r, Q[...], 0.0)
            RS[r : r + 1, :] = -jnp.sum(jnp.sum(found, axis=0), axis=0, keepdims=True)
        out_t[...] = lax.dot_general(
            jnp.ones((out_t.shape[0], LANES), jnp.float32),
            RS[...],
            (((1,), (1,)), ((), ())),
            precision=lax.Precision.HIGHEST,
            preferred_element_type=jnp.float32,
        )

    for n in reversed(range(WINDOW_STEPS)):
        if n == 0:
            terms()
        first, final = n == WINDOW_STEPS - 1, n == 0

        @pl.loop(HALO - n, HALO + X + n)
        def _(x, n=n, first=first, final=final):
            fresh = []
            for part in range(1 if final else 2):
                rows, row = (Y, ro) if final else (YE, 0)
                here = pl.ds(row, rows)
                m = load(MK, (0, part), x, 0, rows, row)
                v = load(U, (n, 0, part), x, 0, rows, row)
                h = EH[n, part, x, here, :]
                s = SG[n, part, x, here, :]
                a = AV[part, x, here, :]
                e = EA[part, x, here, :] if first else AH[part, x, here, :]
                _, flow = spread_of(MU, (n,), x, part, rows, row)
                slope = s * (1.0 - s) * (1.0 / gate_width)
                f_v = h * (2.0 * v - 3.0 * v * v) * (1.0 / tau_inward) - 1.0 / tau_outward
                f_h = v * v * (1.0 - v) * (1.0 / tau_inward)
                g_v = slope * ((h - 1.0) * (1.0 / tau_opening) - h * (1.0 / tau_closing))
                g_h = (s - 1.0) * (1.0 / tau_opening) - s * (1.0 / tau_closing)
                step = step_size * m
                a_new = a + flow + step * (f_v * a + g_v * e)
                e_new = e + step * (f_h * a + g_h * e)
                if final:
                    out_v[x - HALO] = a_new
                    out_h[x - HALO] = e_new
                else:
                    AV[part, x] = a_new
                    AH[part, x] = e_new
                    fresh.append(m * a_new)
            if not final:
                put_kinds(MU, (n - 1,), x, *fresh)


def vmem(n):
    return [pl.BlockSpec(memory_space=pltpu.VMEM)] * n


def local(pot, gat, adv, adh, rec, mask, sec, reg, table, cond):
    X, Y, Z = pot.shape
    size_x, size_y, size_z = (lax.axis_size(a) for a in ("gx", "gy", "gz"))
    assert size_y == 2 and Z == LANES and X >= HALO and Y % TILE == 0 and Y >= TILE
    assert table.shape[0] <= LANES and cond.shape[0] <= SLOT
    mx, mz = matchings(size_x), matchings(size_z)
    nx, nz = len(mx), len(mz)
    f32 = jnp.float32
    block = jax.ShapeDtypeStruct((X, Y, Z), f32)
    packed = pl.pallas_call(
        functools.partial(pack_kernel, nx),
        out_shape=[jax.ShapeDtypeStruct((PLANES, Y, Z), f32)] * nx
        + [block]
        + [jax.ShapeDtypeStruct((HALO, Y, Z), f32)] * nx
        + [jax.ShapeDtypeStruct((6, X, TILE, Z), f32), block, block, block],
        in_specs=[pl.BlockSpec(memory_space=pltpu.SMEM)] + vmem(8),
        out_specs=vmem(2 * nx + 5),
        name="pack",
    )(cond, pot, gat, adv, adh, rec, mask, sec, reg)
    sx, sz, sd = packed[:nx], packed[nx], packed[nx + 1 : 2 * nx + 1]
    sy, g, s, b = packed[2 * nx + 1 :]

    rx = [lax.ppermute(sx[k], "gx", list(enumerate(mx[k]))) for k in range(nx)]
    rz = [lax.ppermute(sz, "gz", list(enumerate(mz[k]))) for k in range(nz)]
    rd = []
    for kx in range(nx):
        for kz in range(nz):
            pairs = [
                (i * size_z + k, mx[kx][i] * size_z + mz[kz][k])
                for i in range(size_x)
                for k in range(size_z)
            ]
            rd.append(lax.ppermute(sd[kx], ("gx", "gz"), pairs))
    swap = [(0, 1), (1, 0)]
    over = lambda arrays: [lax.ppermute(a, "gy", swap) for a in arrays]
    (yo,) = over([sy])
    yx, yz, yd = over(rx), over(rz), over(rd)

    tab = jnp.pad(0.5 * table.T, ((0, 16 - DIRS), (0, LANES - table.shape[0])))
    devices = size_x * size_y * size_z
    XE, YE = X + 2 * HALO, Y + TILE
    rows = XE * (YE + TILE) + 2 * TILE
    pad = lambda *lead: pltpu.VMEM(lead + (2, rows, LANES), f32)
    ext = lambda *lead: pltpu.VMEM(lead + (2, XE, YE, LANES), f32)
    steps = WINDOW_STEPS
    regions = cond.shape[0]
    operands = [tab, reg, pot, g, s, gat, b, adh, *rx, *rz, *rd, yo, *yx, *yz, *yd]
    lam_v, lam_h, tot = pl.pallas_call(
        functools.partial(window_kernel, nx, nz, (size_x, size_z)),
        out_shape=[block, block, jax.ShapeDtypeStruct((devices, LANES), f32)],
        in_specs=vmem(len(operands)),
        out_specs=vmem(3),
        scratch_shapes=[
            pad(steps, 3), pad(steps, 3), pad(3), pad(DIRS), pad(len(Z_DIRS)),
            pad(DIRS), pad(len(Z_DIRS)),
            ext(), ext(), ext(steps), ext(), ext(), ext(steps), ext(), ext(),
            pltpu.VMEM((X, Y, LANES), f32), pltpu.VMEM((LANES, LANES), f32),
        ],
        compiler_params=pltpu.CompilerParams(vmem_limit_bytes=52 << 20),
        name="window",
    )(*operands)
    every = lax.all_to_all(tot.reshape(devices, 1, LANES), ("gx", "gy", "gz"), 0, 0)
    cells = X * Y * Z * devices
    scale = gradient_gain / math.sqrt(cells / regions)
    total = jnp.sum(every, axis=(0, 1))[:regions] * (scale / cond)
    return lam_v, lam_h, total


def solution(mesh):
    cells = P(("twin", "gx"), "gy", "gz")
    in_specs = (cells,) * 8 + (P("twin", None), P("twin"))
    out_specs = (cells, cells, P("twin"))
    return jax.shard_map(local, mesh=mesh, in_specs=in_specs, out_specs=out_specs, check_vma=False)
```

```python
import functools
import math

import jax
import jax.numpy as jnp
from jax import lax
from jax.experimental import pallas as pl
from jax.experimental.pallas import tpu as pltpu
from jax.sharding import PartitionSpec as P

WINDOW_STEPS = 3
HALO = 2 * WINDOW_STEPS
LANES = 128
TILE = 8

step_size = 0.1
tau_inward = 0.3
tau_outward = 6.0
tau_opening = 12.0
tau_closing = 15.0
gate_level = 0.13
gate_width = 0.02
gradient_gain = 30.0
PAIR_OFFSETS = (
    (1, 0, 0),
    (0, 1, 0),
    (0, 0, 1),
    (1, 1, 0),
    (1, -1, 0),
    (1, 0, 1),
    (1, 0, -1),
    (0, 1, 1),
    (0, 1, -1),
)
DIRS = len(PAIR_OFFSETS)
Z_DIRS = tuple(d for d, o in enumerate(PAIR_OFFSETS) if o[2])
Y_DIRS = tuple(d for d, o in enumerate(PAIR_OFFSETS) if o[1])
V, G, S, H, B, A = range(6)
WIDTHS = (HALO, HALO, HALO, HALO - 1, WINDOW_STEPS, WINDOW_STEPS - 1)
STARTS = tuple(sum(WIDTHS[:f]) for f in range(6))
PLANES = sum(WIDTHS)
SLOT = 16


def matchings(count):
    result = []
    for parity in range(0 if count == 1 else 1 if count == 2 else 2):
        partner = [i + 1 if i % 2 == parity else i - 1 for i in range(count)]
        result.append([j if 0 <= j < count else None for j in partner])
    return result


def exchange(array, sizes, along_x=None, along_z=None):
    size_x, size_y, size_z = sizes
    pairs = []
    for i in range(size_x):
        for j in range(size_y):
            for k in range(size_z):
                x = along_x[i] if along_x else i
                z = along_z[k] if along_z else k
                to = (i, 1 - j, k) if x is None or z is None else (x, j, z)
                flat = [(p * size_y + q) * size_z + r for p, q, r in ((i, j, k), to)]
                pairs.append(tuple(flat))
    return lax.ppermute(array, ("gx", "gy", "gz"), pairs)


def looks_up(axis, parity):
    return lax.rem(lax.axis_index(axis), 2) == parity


def lane_ids(rows):
    return lax.broadcasted_iota(jnp.int32, (rows, LANES), 1)


def aligned(start):
    return start if isinstance(start, int) else pl.multiple_of(start, TILE)


def pack_kernel(nx, *refs):
    sources, outs, scratch = refs[:9], refs[9:-10], refs[-10:]
    sx, sz, sd = outs[:nx], outs[nx], outs[nx + 1 : 2 * nx + 1]
    sy, g_out, s_out, b_out = outs[2 * nx + 1 :]
    pot, gat, adh, reg, adv, rec, mask, sec, cond, landed = scratch
    copies = [
        pltpu.make_async_copy(source, place, landed.at[i])
        for i, (source, place) in enumerate(
            zip(sources, (pot, gat, adv, adh, rec, mask, sec, reg, cond), strict=True)
        )
    ]
    for i in (8, 5, 7, 6, 2, 4, 0, 1, 3):
        copies[i].start()
    X, Y, _ = pot.shape
    core = lax.axis_index("gy")
    for i in (8, 5, 7):
        copies[i].wait()
    label = reg[...]
    factor = jnp.zeros(label.shape, jnp.float32)
    for r in range(cond.shape[0]):
        factor = jnp.where(label == r, cond[r], factor)
    m = mask[...].astype(jnp.float32)
    g_out[...] = m * factor
    copies[6].wait()
    s_out[...] = sec[...].astype(jnp.float32)
    copies[2].wait()
    copies[4].wait()
    b_out[...] = adv[...] - m * rec[...]
    for i in (0, 1, 3):
        copies[i].wait()
    fields = (pot, g_out, s_out, gat, b_out, adh)
    for k in range(nx):
        up = looks_up("gx", k)
        for f, w in enumerate(WIDTHS):
            start = jnp.where(up, X - w, 0)
            sx[k][STARTS[f] : STARTS[f] + w] = fields[f][pl.ds(start, w)]
    lanes = lane_ids(X * Y)
    packed = pot[...].reshape(X * Y, LANES)
    for f in range(1, 6):
        rolled = pltpu.roll(fields[f][...].reshape(X * Y, LANES), SLOT * f, 1)
        inside = (lanes >= SLOT * f - SLOT // 2) & (lanes < SLOT * f + SLOT // 2)
        packed = jnp.where(inside, rolled, packed)
    sz[...] = packed.reshape(X, Y, LANES)
    for k in range(nx):
        start = jnp.where(looks_up("gx", k), X - HALO, 0)
        sd[k][...] = sz[pl.ds(start, HALO)]
    row = pl.multiple_of(jnp.where(core == 0, Y - TILE, 0), TILE)
    for f in range(6):
        sy[f] = fields[f][:, pl.ds(row, TILE), :]


def z_up(a, h):
    last = lane_ids(a.shape[0]) == LANES - 1
    ra, rh = pltpu.roll(a, LANES - 1, 1), pltpu.roll(h, LANES - 1, 1)
    return jnp.where(last, rh, ra), jnp.where(last, ra, rh)


def z_down(a, h):
    first = lane_ids(a.shape[0]) == 0
    ra, rh = pltpu.roll(a, 1, 1), pltpu.roll(h, 1, 1)
    return jnp.where(first, rh, ra), jnp.where(first, ra, rh)


def window_kernel(nx, nz, sizes, *refs):
    size_x, size_z = sizes
    it = iter(refs)

    def take(n):
        return [next(it) for _ in range(n)]

    tab, reg = take(2)
    own = take(6)
    rx, rz, rd = take(nx), take(nz), take(nx * nz)
    (yo,) = take(1)
    yx, yz, yd = take(nx), take(nz), take(nx * nz)
    out_v, out_h, out_t = take(3)
    U, MU = take(WINDOW_STEPS), take(WINDOW_STEPS)
    MK, FL, FZ, K, KZ = take(5)
    EH, SG = take(WINDOW_STEPS), take(WINDOW_STEPS)
    EG, ES, EB, EA, AV, AH, D, Q, RS = take(9)

    X, Y, _ = own[V].shape
    XE, YE = X + 2 * HALO, Y + TILE
    ROW = YE + TILE
    core = lax.axis_index("gy")
    xi, zi = lax.axis_index("gx"), lax.axis_index("gz")
    ro = pl.multiple_of(TILE * core, TILE)
    po = pl.multiple_of(Y * (1 - core), TILE)
    ps = pl.multiple_of((Y - TILE) * core, TILE)

    def at(x, row=0):
        return aligned(x * ROW + TILE + row)

    def load(ref, index, x, dy=0, rows=None, row=0):
        start = x * ROW + TILE + row + dy
        if not dy:
            start = aligned(start)
        return ref[index + (pl.ds(start, rows or YE), slice(None))]

    blank = jnp.zeros((TILE, LANES), jnp.float32)

    @pl.loop(0, XE + 1)
    def _(x):
        row = pl.multiple_of(x * ROW, TILE)
        for part in range(2):
            for kind in range(3):
                for n in range(WINDOW_STEPS):
                    U[n][kind, part, pl.ds(row, TILE), :] = blank
                    MU[n][kind, part, pl.ds(row, TILE), :] = blank
                MK[kind, part, pl.ds(row, TILE), :] = blank
            for d in Y_DIRS:
                K[d, part, pl.ds(row, TILE), :] = blank
                FL[d, part, pl.ds(row, TILE), :] = blank
            for i, d in enumerate(Z_DIRS):
                if d in Y_DIRS:
                    KZ[i, part, pl.ds(row, TILE), :] = blank
                    FZ[i, part, pl.ds(row, TILE), :] = blank

    stores = {G: EG, S: ES, H: EH[0], B: EB, A: EA}

    def put(f, part, xe, row, value):
        rows = value.shape[0]
        if f == V:
            U[0][0, part, pl.ds(at(xe, row), rows), :] = value
        else:
            stores[f][part, xe, pl.ds(row, rows), :] = value

    def spread(f, packs):
        parts = [pltpu.roll(p, (LANES - SLOT * f) % LANES, 1) if f else p for p in packs]
        if len(parts) == 1:
            value = parts[0]
        else:
            value = jnp.where(lane_ids(parts[0].shape[0]) < LANES // 2, *[
                jnp.where(looks_up("gz", 0), parts[0], parts[1]),
                jnp.where(looks_up("gz", 0), parts[1], parts[0]),
            ])
        return value

    def lanes_ok(rows):
        lanes = lane_ids(rows)
        right = (lanes < HALO) & (zi < size_z - 1)
        left = (lanes >= LANES - HALO) & (zi > 0)
        return right | left

    if nx < 2 or nz < 1:
        for ref in stores.values():
            ref[...] = jnp.zeros(ref.shape, jnp.float32)
        U[0][0] = jnp.zeros(U[0].shape[1:], jnp.float32)

    for f, w in enumerate(WIDTHS):
        for i in range(X):
            put(f, 0, HALO + i, ro, own[f][i])
            put(f, 0, HALO + i, po, yo[f, i])
        for k in range(nx):
            up = looks_up("gx", k)
            ok = jnp.where(up, xi < size_x - 1, xi > 0)
            dest = jnp.where(up, HALO + X, HALO - w)
            for i in range(w):
                mine = rx[k][STARTS[f] + i]
                theirs = yx[k][STARTS[f] + i, pl.ds(ps, TILE), :]
                if f == G:
                    mine, theirs = jnp.where(ok, mine, 0.0), jnp.where(ok, theirs, 0.0)
                put(f, 0, dest + i, ro, mine)
                put(f, 0, dest + i, po, theirs)

    if nz:

        def halo_plane(xe, ok, mine, theirs):
            for f in range(6):
                a, b = spread(f, mine), spread(f, theirs)
                if f == G:
                    a = jnp.where(lanes_ok(Y) & ok, a, 0.0)
                    b = jnp.where(lanes_ok(TILE) & ok, b, 0.0)
                put(f, 1, xe, ro, a)
                put(f, 1, xe, po, b)

        @pl.loop(0, X)
        def _(i):
            halo_plane(
                HALO + i, True, [r[i] for r in rz], [r[i, pl.ds(ps, TILE), :] for r in yz]
            )

        @pl.loop(0, HALO)
        def _(i):
            for k in range(nx):
                up = looks_up("gx", k)
                ok = jnp.where(up, xi < size_x - 1, xi > 0)
                dest = jnp.where(up, HALO + X, 0)
                halo_plane(
                    dest + i,
                    ok,
                    [r[i] for r in rd[k * nz : (k + 1) * nz]],
                    [r[i, pl.ds(ps, TILE), :] for r in yd[k * nz : (k + 1) * nz]],
                )

    def put_kinds(ref, index, x, a, h):
        rows = pl.ds(at(x), YE)
        for kind, (p, q) in enumerate(((a, h), z_up(a, h), z_down(a, h))):
            ref[index + (kind, 0, rows, slice(None))] = p
            ref[index + (kind, 1, rows, slice(None))] = q

    @pl.loop(0, XE)
    def _(x):
        rows = pl.ds(at(x), YE)
        v = [load(U[0], (0, part), x) for part in range(2)]
        for kind, pair in ((1, z_up(*v)), (2, z_down(*v))):
            for part in range(2):
                U[0][kind, part, rows, :] = pair[part]
        g = [EG[part, x] for part in range(2)]
        put_kinds(MK, (), x, *[jnp.where(t > 0.0, 1.0, 0.0) for t in g])
        sector = [
            jnp.where(g[part] > 0.0, ES[part, x], 0.0).astype(jnp.int32) for part in range(2)
        ]
        lines = [jnp.broadcast_to(tab[d : d + 1, :], (TILE, LANES)) for d in range(DIRS)]
        for t in range(0, YE, TILE):
            tile = pl.ds(at(x, t), TILE)
            flux = []
            for part in range(2):
                index = sector[part][t : t + TILE]
                flux.append(
                    [
                        g[part][t : t + TILE] * jnp.take_along_axis(line, index, axis=1)
                        for line in lines
                    ]
                )
                for d in range(DIRS):
                    FL[d, part, tile, :] = flux[part][d]
            for i, d in enumerate(Z_DIRS):
                dz = PAIR_OFFSETS[d][2]
                pair = (z_up if dz > 0 else z_down)(flux[0][d], flux[1][d])
                for part in range(2):
                    FZ[i, part, tile, :] = pair[part]

    def kind_of(dz):
        return 0 if dz == 0 else 1 if dz > 0 else 2

    @pl.loop(0, XE - 1)
    def _(x):
        rows = pl.ds(at(x), YE)
        for d, (dx, dy, dz) in enumerate(PAIR_OFFSETS):
            pair = []
            for part in range(2):
                there = (
                    load(FZ, (Z_DIRS.index(d), part), x + dx, dy)
                    if dz
                    else load(FL, (d, part), x + dx, dy)
                )
                pair.append(
                    load(FL, (d, part), x) * load(MK, (kind_of(dz), part), x + dx, dy)
                    + there * load(MK, (0, part), x)
                )
                K[d, part, rows, :] = pair[part]
            if dz:
                back = (z_down if dz > 0 else z_up)(*pair)
                for part in range(2):
                    KZ[Z_DIRS.index(d), part, rows, :] = back[part]

    def spread_of(u, x, part, rows=None, row=0, fill=False):
        total, couplings = None, None
        for d, (dx, dy, dz) in enumerate(PAIR_OFFSETS):
            for sign in (1, -1):
                if sign > 0:
                    coupling = load(K, (d, part), x, 0, rows, row)
                else:
                    ref, i = (KZ, Z_DIRS.index(d)) if dz else (K, d)
                    coupling = load(ref, (i, part), x - dx, -dy, rows, row)
                term = coupling * load(
                    u, (kind_of(sign * dz), part), x + sign * dx, sign * dy, rows, row
                )
                total = term if total is None else total + term
                if fill:
                    couplings = coupling if couplings is None else couplings + coupling
        here = pl.ds(row, rows or YE)
        if fill:
            D[part, x, here, :] = couplings
        else:
            couplings = D[part, x, here, :]
        centre = load(u, (0, part), x, 0, rows, row)
        return centre, total - couplings * centre

    for n in range(WINDOW_STEPS):
        reach = HALO - 1 - n
        last = n == WINDOW_STEPS - 1

        @pl.loop(HALO - reach, HALO + X + reach, unroll=2)
        def _(x, n=n, last=last):
            fresh = []
            for part in range(2):
                v, flow = spread_of(U[n], x, part, fill=n == 0)
                h = EH[n][part, x]
                s = jax.nn.sigmoid((v - gate_level) * (1.0 / gate_width))
                SG[n][part, x] = s
                rise = (step_size / tau_inward) * (v * v) * (1.0 - v)
                v_new = (v * (1.0 - step_size / tau_outward) + h * rise) + flow
                if last:
                    m = load(MK, (0, part), x)
                    a = EB[part, x] + m * v_new
                    AV[part, x] = a
                    fresh.append(m * a)
                else:
                    rest = s - 1.0
                    EH[n + 1][part, x] = h + (
                        rest * (h - 1.0) * (step_size / tau_opening)
                        - s * h * (step_size / tau_closing)
                    )
                    fresh.append(v_new)
            if last:
                put_kinds(MU[n], (), x, *fresh)
            else:
                put_kinds(U[n + 1], (), x, *fresh)

    def terms():
        row = ro

        @pl.loop(0, X)
        def _(i):
            x = HALO + i
            mu = [load(MU[n], (0, 0), x, 0, Y, row) for n in range(WINDOW_STEPS)]
            v = [load(U[n], (0, 0), x, 0, Y, row) for n in range(WINDOW_STEPS)]
            total = jnp.zeros((Y, LANES), jnp.float32)
            for d, (dx, dy, dz) in enumerate(PAIR_OFFSETS):
                edge = None
                for sign in (1, -1):
                    index = (kind_of(sign * dz), 0)
                    where = (x + sign * dx, sign * dy, Y, row)
                    part = None
                    for n in range(WINDOW_STEPS):
                        term = (load(MU[n], index, *where) - mu[n]) * (
                            load(U[n], index, *where) - v[n]
                        )
                        part = term if part is None else part + term
                    part = part * load(MK, index, *where)
                    edge = part if edge is None else edge + part
                total = total + load(FL, (d, 0), x, 0, Y, row) * edge
            Q[i] = total

        RS[...] = jnp.zeros(RS.shape, jnp.float32)
        label = reg[...]
        for r in range(SLOT):
            found = jnp.where(label == r, Q[...], 0.0)
            RS[r : r + 1, :] = jnp.sum(jnp.sum(found, axis=0), axis=0, keepdims=True)
        sums = lax.dot_general(
            jnp.ones((TILE, LANES), jnp.float32),
            RS[...],
            (((1,), (1,)), ((), ())),
            precision=lax.Precision.HIGHEST,
            preferred_element_type=jnp.float32,
        )
        sums = sums * jnp.broadcast_to(tab[DIRS : DIRS + 1, :], sums.shape)
        for i in range(0, out_t.shape[0], TILE):
            out_t[i : i + TILE] = sums

    for n in reversed(range(WINDOW_STEPS)):
        if n == 0:
            terms()
        first, final = n == WINDOW_STEPS - 1, n == 0

        @pl.loop(HALO - n, HALO + X + n, unroll=2)
        def _(x, n=n, first=first, final=final):
            fresh = []
            for part in range(1 if final else 2):
                rows, row = (Y, ro) if final else (YE, 0)
                here = pl.ds(row, rows)
                m = load(MK, (0, part), x, 0, rows, row)
                v = load(U[n], (0, part), x, 0, rows, row)
                h = EH[n][part, x, here, :]
                s = SG[n][part, x, here, :]
                a = AV[part, x, here, :]
                e = EA[part, x, here, :] if first else AH[part, x, here, :]
                _, flow = spread_of(MU[n], x, part, rows, row)
                in_v = v * (step_size / tau_inward)
                f_v = h * in_v * (2.0 - 3.0 * v) - step_size / tau_outward
                f_h = in_v * v * (1.0 - v)
                open_, close = step_size / tau_opening, step_size / tau_closing
                g_v = s * (1.0 - s) * (
                    h * ((open_ - close) / gate_width) - open_ / gate_width
                )
                g_h = s * (open_ - close) - open_
                a_new = (a + flow) + m * (f_v * a + g_v * e)
                e_new = e + m * (f_h * a + g_h * e)
                if final:
                    out_v[x - HALO] = a_new
                    out_h[x - HALO] = e_new
                else:
                    AV[part, x] = a_new
                    AH[part, x] = e_new
                    fresh.append(m * a_new)
            if not final:
                put_kinds(MU[n - 1], (), x, *fresh)


def vmem(n):
    return [pl.BlockSpec(memory_space=pltpu.VMEM)] * n


def local(pot, gat, adv, adh, rec, mask, sec, reg, table, cond):
    X, Y, Z = pot.shape
    size_x, size_y, size_z = (lax.axis_size(a) for a in ("gx", "gy", "gz"))
    assert size_y == 2 and Z == LANES and X >= HALO and Y % TILE == 0 and Y >= TILE
    assert table.shape[0] <= LANES and cond.shape[0] <= SLOT
    mx, mz = matchings(size_x), matchings(size_z)
    nx, nz = len(mx), len(mz)
    f32 = jnp.float32
    block = jax.ShapeDtypeStruct((X, Y, Z), f32)
    whole = pltpu.VMEM((X, Y, Z), f32)
    args = (pot, gat, adv, adh, rec, mask, sec, reg, cond)
    ints = pltpu.VMEM((X, Y, Z), jnp.int32)
    packed = pl.pallas_call(
        functools.partial(pack_kernel, nx),
        out_shape=[jax.ShapeDtypeStruct((PLANES, Y, Z), f32)] * nx
        + [block]
        + [jax.ShapeDtypeStruct((HALO, Y, Z), f32)] * nx
        + [jax.ShapeDtypeStruct((6, X, TILE, Z), f32)]
        + [block] * 3,
        in_specs=[pl.BlockSpec(memory_space=pltpu.HBM)] * 9,
        out_specs=vmem(2 * nx + 5),
        scratch_shapes=[whole, whole, whole, ints, whole, whole, ints, ints,
            pltpu.SMEM(cond.shape, f32),
            pltpu.SemaphoreType.DMA((9,))],
        compiler_params=pltpu.CompilerParams(vmem_limit_bytes=8 << 20),
        name="pack",
    )(*[pltpu.with_memory_space_constraint(a, pltpu.HBM) for a in args])
    sx, sz, sd = packed[:nx], packed[nx], packed[nx + 1 : 2 * nx + 1]
    sy, g, s, b = packed[2 * nx + 1 :]

    sizes = (size_x, size_y, size_z)
    rx = [exchange(sx[k], sizes, mx[k]) for k in range(nx)]
    rz = [exchange(sz, sizes, None, mz[k]) for k in range(nz)]
    rd = [exchange(sd[i], sizes, mx[i], mz[k]) for i in range(nx) for k in range(nz)]
    swap = [(0, 1), (1, 0)]
    over = lambda arrays: [lax.ppermute(a, "gy", swap) for a in arrays]
    (yo,) = over([sy])
    yx, yz, yd = over(rx), over(rz), over(rd)

    cells = X * Y * Z * size_x * size_y * size_z
    scale = gradient_gain / math.sqrt(cells / cond.shape[0])
    tab = jnp.concatenate(
        [
            jnp.pad(0.5 * table.T, ((0, 0), (0, LANES - table.shape[0]))),
            jnp.pad((-scale / cond)[None], ((0, 0), (0, LANES - cond.shape[0]))),
            jnp.zeros((SLOT - DIRS - 1, LANES), f32),
        ]
    )
    devices = size_x * size_y * size_z
    XE, YE = X + 2 * HALO, Y + TILE
    rows = XE * (YE + TILE) + 2 * TILE
    pad = lambda *lead: pltpu.VMEM(lead + (2, rows, LANES), f32)
    ext = lambda *lead: pltpu.VMEM(lead + (2, XE, YE, LANES), f32)
    steps = WINDOW_STEPS
    operands = [tab, reg, pot, g, s, gat, b, adh, *rx, *rz, *rd, yo, *yx, *yz, *yd]
    lam_v, lam_h, tot = pl.pallas_call(
        functools.partial(window_kernel, nx, nz, (size_x, size_z)),
        out_shape=[block, block, jax.ShapeDtypeStruct((devices, LANES), f32)],
        in_specs=vmem(len(operands)),
        out_specs=vmem(3),
        scratch_shapes=[
            *[pad(3)] * (2 * steps),
            pad(3), pad(DIRS), pad(len(Z_DIRS)), pad(DIRS), pad(len(Z_DIRS)),
            *[ext()] * (2 * steps + 7),
            pltpu.VMEM((X, Y, LANES), f32), pltpu.VMEM((LANES, LANES), f32),
        ],
        compiler_params=pltpu.CompilerParams(vmem_limit_bytes=42 << 20),
        name="window",
    )(*operands)
    every = lax.all_to_all(tot.reshape(devices, 1, LANES), ("gx", "gy", "gz"), 0, 0)
    return lam_v, lam_h, jnp.sum(every, axis=(0, 1))[: cond.shape[0]]


def solution(mesh):
    cells = P(("twin", "gx"), "gy", "gz")
    in_specs = (cells,) * 8 + (P("twin", None), P("twin"))
    out_specs = (cells, cells, P("twin"))
    return jax.shard_map(local, mesh=mesh, in_specs=in_specs, out_specs=out_specs, check_vma=False)
```
